32 devices in a mesh: chain: 8 (over z, x), pts: 4 (over y, core).
Axes of the slice: x: 2, y: 2, z: 4, core: 2. Of those that a mesh axis runs over, the one named last changes fastest.
Arguments:
- cam_jac: bfloat16 [2048, 12, 512], P(('chain', 'pts')), may hold values from -0.125 to 0.125
- point_jac: bfloat16 [2048, 6, 512], P(('chain', 'pts')), may hold values from -1.5 to 1.5
- residual: float32 [2048, 2, 512], P(('chain', 'pts')), may hold values from -6 to 6
- obs_cam: int32 [2048, 8], P(('chain', 'pts')), may hold values from 0 to 63, all different within a row; in each aligned block of 64 rows (0 to 63, 64 to 127, ...) at most 8 rows name the same one
- damp_exp: int32 [2, 64], replicated, may hold values from -3 to 0
- cam_step: float32 [64, 384], P('chain'), may hold values from -6 to 6
- diag_inverse: bfloat16 [64, 384, 384], P('chain'), may hold values from -0.06 to 0.56
- coupling: bfloat16 [64, 384, 384], P('chain'), may hold values from -33 to 9
Outputs:
- cam_out: float32 [64, 384], P('chain')
- point_out: float32 [2048, 3, 64], P(('chain', 'pts'))
The draws below stay inside these ranges and needn't reach their ends.
Inputs may be any that keep to these rules, and one draw needn't show every extreme that they name: `obs_cam`: in the point blocks of one device no camera block is named by more than 8 of them, and some camera block is named by exactly 8; each row names 8 different camera blocks, and every camera block is named somewhere.
All inputs are finite; a program needn't handle non-finite values.
Results may differ from the reference program's by a relative error of at most 0.0003.
Values sent between devices are 32-bit elements; how exact they have to be, the bound alone decides.
A program may use at most 192 MiB of HBM per device.

```python
import math
import jax
import jax.numpy as jnp
import numpy as np
from jax import lax

BLOCK = 64
TOP = 8
ITERS = 2
PBD = 64
CVEC = 384
NCB = 64
NPB = 2048
OBS_CAM = 256
MOST = 8


def unit_matrix():
    rows_idx = lax.broadcasted_iota(jnp.int32, (CVEC, CVEC), 0)
    cols_idx = lax.broadcasted_iota(jnp.int32, (CVEC, CVEC), 1)
    return (rows_idx == cols_idx).astype(jnp.float32)


def off_noise(noise_key, spread):
    full_shape = (NCB, CVEC, CVEC)
    values = jnp.clip(jax.random.normal(noise_key, full_shape, jnp.float32), -4.0, 4.0)
    return values * (spread / math.sqrt(CVEC))


def draw_diag_inverse(key, part):
    base_key = jax.random.fold_in(key, 17)
    diag_key, noise_key = jax.random.split(base_key)
    panel_scale = math.sqrt(2.0 / NCB)
    diagonal = jax.random.uniform(diag_key, (NCB, CVEC), jnp.float32, 0.9, 1.1)
    unit = unit_matrix()
    return (panel_scale * (off_noise(noise_key, 0.25) * (1.0 - unit) + unit * diagonal[:, :, None])).astype(jnp.bfloat16)


def draw_coupling(key, part):
    base_key = jax.random.fold_in(key, 29)
    diag_key, noise_key = jax.random.split(base_key)
    panel_scale = math.sqrt(NCB / 2.0)
    kept_share = 0.25
    block_gain = kept_share ** (2.0 / NCB)
    centre = math.sqrt((block_gain - 0.0625) / ((1.0 + 0.01 / 3.0 + 0.0625) * (1.0 + 0.01 / 12.0)))
    diagonal = jax.random.uniform(diag_key, (NCB, CVEC), jnp.float32, 0.95 * centre, 1.05 * centre)
    unit = unit_matrix()
    return (-panel_scale * (off_noise(noise_key, 0.25) * (1.0 - unit) + unit * diagonal[:, :, None])).astype(jnp.bfloat16)


def set_ends(array, rng, low, high):
    shape = array.shape
    index_at = [jax.random.randint(jax.random.fold_in(rng, axis), (), 0, shape[axis]) for axis in range(len(shape))]
    array = array.at[tuple(index_at)].set(low)
    longest = shape.index(max(shape))
    index_at[longest] = (index_at[longest] + 1) % shape[longest]
    return array.at[tuple(index_at)].set(high)


def level_of(key, shape, cuts, smallest, largest):
    factor_of, own = 1.0, jax.random.fold_in(key, 6)
    for dim, shards_of in cuts:
        draws = jnp.exp(jax.random.uniform(jax.random.fold_in(own, dim), (shards_of,), jnp.float32, smallest / len(cuts), largest / len(cuts)))
        factor_of = factor_of * jnp.repeat(draws, shape[dim] // shards_of).reshape([-1 if axis == dim else 1 for axis in range(len(shape))])
    return factor_of


def shared_out(rng, own, number, rows, count, top, most, slope):
    ranking = jax.random.permutation(rng, count)
    heavy_load, usual = portions_of(count, rows * top, most, slope, True), portions_of(count, rows * top, most, slope, False)
    places = jnp.arange(count)

    def named(tallies, turn):
        used = int((tallies > 0).sum())
        fixed = max(1, used // 4)
        shifted = fixed + (places - fixed + turn * (used - fixed)) % max(1, count - fixed)
        return jnp.zeros((count,), jnp.int32).at[ranking[jnp.where(places < fixed, places, shifted)]].set(jnp.asarray(tallies, jnp.int32))

    tallies = jnp.where(number % 4 == 0, named(heavy_load, number // 4), named(usual, number - number // 4 - 1))
    mixed = jax.random.permutation(jax.random.fold_in(own, 3), count)
    giver, sink = mixed[0:count // 2 * 2:2], mixed[1:count // 2 * 2:2]
    room = jnp.minimum(tallies[giver] - 1, most - tallies[sink]) // 2
    room = jnp.where((giver == ranking[0]) | (sink == ranking[0]) | (tallies[sink] == 0), 0, jnp.maximum(room, 0))
    shifted = jax.random.randint(jax.random.fold_in(own, 4), (count // 2,), 0, 1 << 20) % (room + 1)
    tallies = tallies.at[giver].add(-shifted).at[sink].add(shifted)
    labels = jnp.searchsorted(jnp.cumsum(tallies), jnp.arange(rows * top), side="right").astype(jnp.int32)
    table = labels.reshape(top, rows).T
    table = table[jax.random.permutation(jax.random.fold_in(own, 1), rows)]
    turn = jax.random.randint(jax.random.fold_in(own, 2), (rows, 1), 0, top)
    return jnp.take_along_axis(table, (jnp.arange(top)[None, :] + turn) % top, axis=1)


def portions_of(number_of, total, bound, slope, full):
    loads = [(1 << 20) // math.isqrt(standing ** slope) + 1 for standing in range(1, number_of + 1)]
    largest = bound if full else min(bound, max(-(-total // number_of), total * loads[0] // sum(loads)))
    least = 1 if total - largest >= number_of - 1 else 0
    holding, rest = [largest] + [least] * (number_of - 1), total - largest - least * (number_of - 1)
    while rest > 0:
        candidates = [i for i in range(1, number_of) if holding[i] < largest] or [i for i in range(1, number_of) if holding[i] < bound]
        mass, budget = sum([loads[i] for i in candidates]), rest
        for i in candidates:
            more = min(bound - holding[i], max(1, budget * loads[i] // mass), rest)
            holding[i] = holding[i] + more
            rest = rest - more
    return np.array(holding)


def scatter_about(rng, dims, width, reach, cuts=(), kind=jnp.bfloat16):
    loudness = level_of(rng, dims, cuts, -0.22, 0.18) if cuts else 1.0
    values = jax.random.normal(rng, dims, jnp.float32) * width * loudness
    return jnp.minimum(jnp.maximum(values, -reach), reach).astype(kind)


def setup_inputs(seed: int = 0) -> dict:
    streams_of = jax.random.split(jax.random.key(seed), 9)
    cam_jac = scatter_about(streams_of[0], (NPB, 12, TOP * BLOCK), (8 * OBS_CAM) ** -0.5, 0.125, ((0, 32),))
    point_jac = scatter_about(streams_of[1], (NPB, 6, TOP * BLOCK), (2 * TOP) ** -0.5, 1.5, ((0, 32),))
    residual = scatter_about(streams_of[2], (NPB, 2, TOP * BLOCK), 1.0, 6.0, ((0, 32),), jnp.float32)
    obs_cam_keys = jax.random.split(jax.random.fold_in(streams_of[3], 1), NPB // PBD)
    obs_cam_turns = jax.random.permutation(jax.random.fold_in(streams_of[3], 3), NPB // PBD)
    obs_cam = jax.vmap(lambda own, number: shared_out(jax.random.fold_in(streams_of[3], 2), own, number, PBD, NCB, TOP, MOST, 2))(obs_cam_keys, obs_cam_turns).reshape((NPB, TOP))
    damp_exp = set_ends(jax.random.randint(streams_of[4], (ITERS, BLOCK), -3, 1), jax.random.fold_in(streams_of[4], 1), -3, 0).astype(jnp.int32)
    cam_step = scatter_about(streams_of[5], (NCB, CVEC), 1.0, 6.0, ((0, 8),), jnp.float32)
    diag_inverse = draw_diag_inverse(jax.random.fold_in(streams_of[8], 71), 0)
    coupling = draw_coupling(jax.random.fold_in(streams_of[8], 71), 0)
    return {"cam_jac": cam_jac, "point_jac": point_jac, "residual": residual, "obs_cam": obs_cam, "damp_exp": damp_exp, "cam_step": cam_step, "diag_inverse": diag_inverse, "coupling": coupling}


exact_mode = lax.Precision.HIGHEST


def solve_three(hessian, target):
    aa_entry = hessian[:, 0, 0]
    ab_entry = hessian[:, 0, 1]
    ac_entry = hessian[:, 0, 2]
    bb_entry = hessian[:, 1, 1]
    bc_entry = hessian[:, 1, 2]
    cc_entry = hessian[:, 2, 2]
    cof_aa = bb_entry * cc_entry - bc_entry * bc_entry
    cof_ab = ac_entry * bc_entry - ab_entry * cc_entry
    cof_ac = ab_entry * bc_entry - ac_entry * bb_entry
    cof_bb = aa_entry * cc_entry - ac_entry * ac_entry
    cof_bc = ab_entry * ac_entry - aa_entry * bc_entry
    cof_cc = aa_entry * bb_entry - ab_entry * ab_entry
    determinant = aa_entry * cof_aa + ab_entry * cof_ab + ac_entry * cof_ac
    component_a = (cof_aa * target[:, 0] + cof_ab * target[:, 1] + cof_ac * target[:, 2]) / determinant
    component_b = (cof_ab * target[:, 0] + cof_bb * target[:, 1] + cof_bc * target[:, 2]) / determinant
    component_c = (cof_ac * target[:, 0] + cof_bc * target[:, 1] + cof_cc * target[:, 2]) / determinant
    return jnp.stack([component_a, component_b, component_c], axis=1)


def eliminate(cam_jac, point_jac, residual, obs_cam, cam_all, damping):
    blocks, observers = obs_cam.shape
    span_width = residual.shape[2]
    per_block = span_width // observers
    gathered = cam_all[obs_cam.reshape(-1)]
    cam_values = gathered.reshape(blocks, observers, 6, per_block).transpose(0, 2, 1, 3).reshape(blocks, 6, span_width)
    cam_terms = cam_jac.astype(jnp.float32).reshape(blocks, 2, 6, span_width)
    misfit = residual + jnp.sum(cam_terms * cam_values[:, None], axis=2)
    point_terms = point_jac.astype(jnp.float32).reshape(blocks, 2, 3, observers, per_block)
    misfit_obs = misfit.reshape(blocks, 2, observers, per_block)
    unit_three = (lax.broadcasted_iota(jnp.int32, (3, 3), 0) == lax.broadcasted_iota(jnp.int32, (3, 3), 1)).astype(jnp.float32)
    hessian = jnp.sum(point_terms[:, :, :, None] * point_terms[:, :, None, :], axis=(1, 4)) + unit_three[None, :, :, None] * damping[None, None, None, :]
    target = jnp.sum(point_terms * misfit_obs[:, :, None], axis=(1, 3))
    solution = solve_three(hessian, target)
    projected = misfit_obs - jnp.sum(point_terms * solution[:, None, :, None, :], axis=2)
    adjoint = jnp.sum(cam_terms * projected.reshape(blocks, 2, 1, span_width), axis=1)
    adjoint = adjoint.reshape(blocks, 6, observers, per_block).transpose(0, 2, 1, 3).reshape(blocks * observers, 6 * per_block)
    return adjoint, solution


def apply_panels(gradient, diag_inverse, coupling):
    cam_width = gradient.shape[1]

    def advance(carried, panels):
        inverse_block, coupling_block, grad_block = panels
        inverse_wide = inverse_block.astype(jnp.float32)
        coupling_wide = coupling_block.astype(jnp.float32)
        solved = jnp.dot(inverse_wide.T, grad_block - carried, precision=exact_mode)
        return jnp.dot(coupling_wide.T, solved, precision=exact_mode), solved

    _, solved_all = lax.scan(advance, jnp.zeros((cam_width,), jnp.float32), (diag_inverse, coupling, gradient))

    def retreat(later, panels):
        inverse_block, coupling_block, solved_block = panels
        inverse_wide = inverse_block.astype(jnp.float32)
        coupling_wide = coupling_block.astype(jnp.float32)
        update = jnp.dot(inverse_wide, solved_block - jnp.dot(coupling_wide, later, precision=exact_mode), precision=exact_mode)
        return update, update

    _, updates = lax.scan(retreat, jnp.zeros((cam_width,), jnp.float32), (diag_inverse, coupling, solved_all), reverse=True)
    return updates


def reference(cam_jac, point_jac, residual, obs_cam, damp_exp, cam_step, diag_inverse, coupling):
    total_blocks = cam_step.shape[0]
    flat_ids = obs_cam.reshape(-1)
    dampings = jnp.exp2(damp_exp.astype(jnp.float32))
    camera = cam_step
    for iteration in range(ITERS):
        damp_row = dampings[iteration]
        adjoint, _ = eliminate(cam_jac, point_jac, residual, obs_cam, camera, damp_row)
        cam_damp = jnp.tile(damp_row, 6)
        gradient = jax.ops.segment_sum(adjoint, flat_ids, num_segments=total_blocks) + cam_damp[None, :] * camera
        camera = camera - apply_panels(gradient, diag_inverse, coupling)
    _, solution = eliminate(cam_jac, point_jac, residual, obs_cam, camera, dampings[ITERS - 1])
    return camera, -solution
```

```python
import functools

import jax
import jax.numpy as jnp
from jax import lax
from jax.experimental import pallas as pl
from jax.experimental.pallas import tpu as pltpu
from jax.sharding import PartitionSpec as P

ITERS = 2
MESH = pl.DeviceIdType.MESH
F32, BF16 = jnp.float32, jnp.bfloat16
VMEM = pl.BlockSpec(memory_space=pltpu.VMEM)
ANY = pl.BlockSpec(memory_space=pl.ANY)


def dot_rows(x, panel):
    return lax.dot_general(x, panel, (((1,), (0,)), ((), ())), preferred_element_type=F32)


def dot_cols(x, panel):
    return lax.dot_general(x, panel, (((1,), (1,)), ((), ())), preferred_element_type=F32)


def halves(x):
    high = x.astype(BF16)
    return high, (x - high.astype(F32)).astype(BF16)


def thirds(x):
    high = x.astype(BF16)
    rest = x - high.astype(F32)
    mid = rest.astype(BF16)
    return high, mid, (rest - mid.astype(F32)).astype(BF16)


def maps_kernel(
    df_ref, cf_ref, db_ref, cb_ref, wh_ref, wl_ref, xh_ref, xl_ref, rh_ref, rl_ref, run_f, run_b
):
    @pl.when(pl.program_id(0) == 0)
    def _():
        width = run_f.shape[0]
        unit = (
            lax.broadcasted_iota(jnp.int32, (width, width), 0)
            == lax.broadcasted_iota(jnp.int32, (width, width), 1)
        ).astype(F32)
        run_f[...] = unit
        run_b[...] = unit

    high, low = halves(run_f[...])
    solved = -(dot_rows(high, df_ref[0]) + dot_rows(low, df_ref[0]))
    high, low = halves(solved)
    wh_ref[0] = high
    wl_ref[0] = low
    run_f[...] = dot_rows(high, cf_ref[0]) + dot_rows(low, cf_ref[0])
    high, low = halves(run_b[...])
    misfit = -(dot_cols(high, cb_ref[0]) + dot_cols(low, cb_ref[0]))
    high, low = halves(misfit)
    update = dot_cols(high, db_ref[0]) + dot_cols(low, db_ref[0])
    run_b[...] = update
    high, low = halves(update)
    xh_ref[0] = high
    xl_ref[0] = low

    @pl.when(pl.program_id(0) == pl.num_programs(0) - 1)
    def _():
        high, low = halves(run_f[...])
        rh_ref[...] = high
        rl_ref[...] = low


def sweep_maps(diag_inverse, coupling):
    count, width, _ = diag_inverse.shape
    ahead = pl.BlockSpec((1, width, width), lambda k: (k, 0, 0))
    back = pl.BlockSpec((1, width, width), lambda k: (count - 1 - k, 0, 0))
    whole = pl.BlockSpec((width, width), lambda k: (0, 0))
    stack = jax.ShapeDtypeStruct((count, width, width), BF16)
    one = jax.ShapeDtypeStruct((width, width), BF16)
    return pl.pallas_call(
        maps_kernel,
        grid=(count,),
        in_specs=[ahead, ahead, back, back],
        out_specs=[ahead, ahead, back, back, whole, whole],
        out_shape=[stack, stack, stack, stack, one, one],
        scratch_shapes=[pltpu.VMEM((width, width), F32)] * 2,
        compiler_params=pltpu.CompilerParams(vmem_limit_bytes=32 << 20),
        name="sweep_maps",
    )(diag_inverse, coupling, diag_inverse, coupling)


def eliminate_kernel(adjoint_out, *refs):
    if adjoint_out:
        cam_ref, pick_ref, pick_t_ref, cj_ref, pj_ref, res_ref, damp_ref, out_ref, seen, parts = refs
    else:
        cam_ref, pick_ref, cj_ref, pj_ref, res_ref, damp_ref, out_ref, seen = refs
    rows = res_ref.shape[1]
    blocks = rows // 4
    high, mid, low = thirds(cam_ref[...])
    pick = pick_ref[...]
    seen[...] = (dot_rows(pick, low) + dot_rows(pick, mid)) + dot_rows(pick, high)
    step = 16
    left = lax.broadcasted_iota(jnp.int32, (step, 128), 1) < 64
    damp = damp_ref[...]

    def swap(x):
        return pltpu.roll(x, 64, 1)

    def chunk(i, carry):
        at = pl.multiple_of(i * step, step)
        misfits, points = [], []
        hess = [None] * 6
        target = [None] * 3
        pairs = ((0, 0), (0, 1), (0, 2), (1, 1), (1, 2), (2, 2))
        for tp in range(4):
            here = pl.ds(tp * blocks + at, step)
            there = pl.ds(rows + tp * blocks + at, step)
            cams = []
            for c in range(3):
                even = seen[here, c * 128 : (c + 1) * 128]
                odd = seen[there, c * 128 : (c + 1) * 128]
                cams.append(jnp.where(left, even, swap(odd)))
                cams.append(jnp.where(left, swap(even), odd))
            for a in range(2):
                miss = res_ref[a, here, :]
                for m in range(6):
                    miss = miss + cj_ref[6 * a + m, here, :].astype(F32) * cams[m]
                terms = [pj_ref[3 * a + n, here, :].astype(F32) for n in range(3)]
                misfits.append(miss)
                points.append(terms)
                for e, (n, k) in enumerate(pairs):
                    new = terms[n] * terms[k]
                    hess[e] = new if hess[e] is None else hess[e] + new
                for n in range(3):
                    new = terms[n] * miss
                    target[n] = new if target[n] is None else target[n] + new
        hess = [h + swap(h) for h in hess]
        ta, tb, tc = [t + swap(t) for t in target]
        aa, ab, ac, bb, bc, cc = hess
        aa, bb, cc = aa + damp, bb + damp, cc + damp
        cof_aa = bb * cc - bc * bc
        cof_ab = ac * bc - ab * cc
        cof_ac = ab * bc - ac * bb
        cof_bb = aa * cc - ac * ac
        cof_bc = ab * ac - aa * bc
        cof_cc = aa * bb - ab * ab
        det = aa * cof_aa + ab * cof_ab + ac * cof_ac
        sol = (
            (cof_aa * ta + cof_ab * tb + cof_ac * tc) / det,
            (cof_ab * ta + cof_bb * tb + cof_bc * tc) / det,
            (cof_ac * ta + cof_bc * tb + cof_cc * tc) / det,
        )
        if not adjoint_out:
            for n in range(3):
                out_ref[n, pl.ds(at, step), :] = -sol[n]
            return carry
        for tp in range(4):
            here = pl.ds(tp * blocks + at, step)
            there = pl.ds(rows + tp * blocks + at, step)
            left_over = []
            for a in range(2):
                terms = points[2 * tp + a]
                left_over.append(
                    misfits[2 * tp + a]
                    - (terms[0] * sol[0] + terms[1] * sol[1] + terms[2] * sol[2])
                )
            adj = [
                cj_ref[m, here, :].astype(F32) * left_over[0]
                + cj_ref[6 + m, here, :].astype(F32) * left_over[1]
                for m in range(6)
            ]
            for c in range(3):
                span = slice(c * 128, (c + 1) * 128)
                even = jnp.where(left, adj[2 * c], swap(adj[2 * c + 1]))
                odd = jnp.where(left, swap(adj[2 * c]), adj[2 * c + 1])
                for part, value in enumerate(thirds(even)):
                    parts[part, here, span] = value
                for part, value in enumerate(thirds(odd)):
                    parts[part, there, span] = value
        return carry

    lax.fori_loop(0, blocks // step, chunk, 0)
    if adjoint_out:
        pick_t = pick_t_ref[...]
        out_ref[...] = (
            dot_rows(pick_t, parts[2]) + dot_rows(pick_t, parts[1])
        ) + dot_rows(pick_t, parts[0])


def eliminate(cam_all, pick, pick_t, cj, pj, res, damp, adjoint_out):
    rows, width = res.shape[1], cam_all.shape[1]
    scratch = [pltpu.VMEM((2 * rows, width), F32)]
    if adjoint_out:
        args = (cam_all, pick, pick_t, cj, pj, res, damp)
        out = jax.ShapeDtypeStruct(cam_all.shape, F32)
        scratch.append(pltpu.VMEM((3, 2 * rows, width), BF16))
    else:
        args = (cam_all, pick, cj, pj, res, damp)
        out = jax.ShapeDtypeStruct((3, rows // 4, 128), F32)
    return pl.pallas_call(
        functools.partial(eliminate_kernel, adjoint_out),
        in_specs=[VMEM] * len(args),
        out_specs=VMEM,
        out_shape=out,
        scratch_shapes=scratch,
        compiler_params=pltpu.CompilerParams(vmem_limit_bytes=40 << 20),
        name="eliminate",
    )(*args)


def split_row(v):
    row = lax.broadcasted_iota(jnp.int32, v.shape, 0)
    high = v.astype(BF16).astype(F32)
    rest = v - high
    mid = rest.astype(BF16).astype(F32)
    low = rest - mid
    return jnp.where(row == 0, high, jnp.where(row == 1, mid, jnp.where(row == 2, low, 0.0))).astype(BF16)


def total(y):
    return jnp.broadcast_to(jnp.sum(y, axis=0, keepdims=True), y.shape)


def times(v, panel):
    return total(dot_rows(split_row(v), panel))


def times_t(v, panel):
    return total(dot_cols(split_row(v), panel))


def solve_kernel(
    n_c, n_p,
    dense_ref, cam_ref, damp_ref, d_hbm, c_hbm, wh_hbm, wl_hbm, xh_hbm, xl_hbm, rh_ref, rl_ref,
    own_ref, all_ref,
    d_ref, c_ref, wh_ref, wl_ref, xh_ref, xl_ref,
    landed, piece, grad, solved, carry_in, carry_out, later_in, later_out,
    load_sem, rs_send, rs_recv, pts_send, pts_recv, ring_send, ring_recv, all_send, all_recv,
):
    me_c, me_p = lax.axis_index("chain"), lax.axis_index("pts")
    n = n_c * n_p
    me = me_c * n_p + me_p
    count = cam_ref.shape[0]
    share = count // n_p

    loads = [
        pltpu.make_async_copy(src, dst, load_sem.at[i])
        for i, (src, dst) in enumerate(
            ((d_hbm, d_ref), (c_hbm, c_ref), (wh_hbm, wh_ref), (wl_hbm, wl_ref), (xh_hbm, xh_ref), (xl_hbm, xl_ref))
        )
    ]
    for load in loads:
        load.start()

    barrier = pltpu.get_barrier_semaphore()

    @pl.loop(1, n)
    def _(i):
        to = lax.rem(me + i, n)
        pl.semaphore_signal(
            barrier, inc=1, device_id=(to // n_p, lax.rem(to, n_p)), device_id_type=MESH
        )

    pl.semaphore_wait(barrier, n - 1)

    def rs_copy(i):
        to = lax.rem(me + i, n)
        return pltpu.make_async_remote_copy(
            src_ref=dense_ref.at[to],
            dst_ref=landed.at[i],
            send_sem=rs_send.at[i],
            recv_sem=rs_recv.at[i],
            device_id=(to // n_p, lax.rem(to, n_p)),
            device_id_type=MESH,
        )

    @pl.loop(1, n)
    def _(i):
        rs_copy(i).start()

    landed[0] = dense_ref[me]

    @pl.loop(1, n)
    def _(i):
        rs_copy(i).wait_recv()

    piece[...] = jnp.sum(landed[...], axis=0)

    def pts_copy(i):
        return pltpu.make_async_remote_copy(
            src_ref=piece,
            dst_ref=grad.at[me_p],
            send_sem=pts_send.at[i],
            recv_sem=pts_recv.at[i],
            device_id=(me_c, lax.rem(me_p + i, n_p)),
            device_id_type=MESH,
        )

    for i in range(1, n_p):
        pts_copy(i).start()
    grad[me_p] = piece[...]
    for i in range(1, n_p):
        pts_copy(i).wait_recv()

    damp = damp_ref[...]
    for load in loads[:2]:
        load.wait()

    carried = None
    shape = carry_in.shape
    for k in range(count):
        g = grad[k // share, k % share : k % share + 1, :] + damp * cam_ref[k : k + 1, :]
        g = jnp.broadcast_to(g, shape)
        s = times(g if carried is None else g - carried, d_ref[k])
        solved[k : k + 1, :] = s[0:1]
        carried = times(s, c_ref[k])

    ring_f = pltpu.make_async_remote_copy(
        src_ref=carry_out, dst_ref=carry_in, send_sem=ring_send.at[0], recv_sem=ring_recv.at[0],
        device_id=(lax.rem(me_c + 1, n_c), me_p), device_id_type=MESH,
    )

    @pl.when(me_c == 0)
    def _():
        carry_in[...] = jnp.zeros_like(carry_in)

    @pl.when(me_c > 0)
    def _():
        ring_f.wait_recv()

    x = split_row(carry_in[...])
    carry_out[...] = carried + total(dot_rows(x, rh_ref[...]) + dot_rows(x, rl_ref[...]))

    @pl.when(me_c < n_c - 1)
    def _():
        ring_f.start()

    for load in loads[2:4]:
        load.wait()
    for k in range(count):
        y = dot_rows(x, wh_ref[k]) + dot_rows(x, wl_ref[k])
        solved[k : k + 1, :] = solved[k : k + 1, :] + jnp.sum(y, axis=0, keepdims=True)

    later = None
    updates = [None] * count
    for k in reversed(range(count)):
        r = jnp.broadcast_to(solved[k : k + 1, :], shape)
        if later is not None:
            r = r - times_t(later, c_ref[k])
        later = times_t(r, d_ref[k])
        updates[k] = later[0:1]

    ring_b = pltpu.make_async_remote_copy(
        src_ref=later_out, dst_ref=later_in, send_sem=ring_send.at[1], recv_sem=ring_recv.at[1],
        device_id=(lax.rem(me_c + n_c - 1, n_c), me_p), device_id_type=MESH,
    )

    for load in loads[4:]:
        load.wait()

    @pl.when(me_c == n_c - 1)
    def _():
        later_in[...] = jnp.zeros_like(later_in)

    @pl.when(me_c < n_c - 1)
    def _():
        ring_b.wait_recv()

    x = split_row(later_in[...])
    later_out[...] = later + total(dot_rows(x, xh_ref[0]) + dot_rows(x, xl_ref[0]))

    @pl.when(me_c > 0)
    def _():
        ring_b.start()

    for k in range(count):
        y = dot_rows(x, xh_ref[k]) + dot_rows(x, xl_ref[k])
        own_ref[k : k + 1, :] = cam_ref[k : k + 1, :] - (updates[k] + jnp.sum(y, axis=0, keepdims=True))

    def all_copy(i):
        return pltpu.make_async_remote_copy(
            src_ref=own_ref,
            dst_ref=all_ref.at[me_c],
            send_sem=all_send.at[i],
            recv_sem=all_recv.at[i],
            device_id=(lax.rem(me_c + i, n_c), me_p),
            device_id_type=MESH,
        )

    @pl.loop(1, n_c)
    def _(i):
        all_copy(i).start()

    all_ref[me_c] = own_ref[...]

    @pl.loop(1, n_c)
    def _(i):
        all_copy(i).wait()

    @pl.loop(1, n)
    def _(i):
        rs_copy(i).wait_send()

    for i in range(1, n_p):
        pts_copy(i).wait_send()

    @pl.when(me_c < n_c - 1)
    def _():
        ring_f.wait_send()

    @pl.when(me_c > 0)
    def _():
        ring_b.wait_send()


def solve(n_c, n_p, dense, camera, damp, diag_inverse, coupling, maps):
    count, width = camera.shape
    n = n_c * n_p
    share = count // n_p
    wh, wl, xh, xl, rh, rl = maps
    panel = pltpu.VMEM((count, width, width), BF16)
    vec = pltpu.VMEM((8, width), F32)
    sem = pltpu.SemaphoreType.DMA
    own, everyone = pl.pallas_call(
        functools.partial(solve_kernel, n_c, n_p),
        in_specs=[VMEM, VMEM, VMEM, ANY, ANY, ANY, ANY, ANY, ANY, VMEM, VMEM],
        out_specs=[VMEM, VMEM],
        out_shape=[
            jax.ShapeDtypeStruct((count, width), F32),
            jax.ShapeDtypeStruct((n_c, count, width), F32),
        ],
        scratch_shapes=[panel] * 6
        + [
            pltpu.VMEM((n, share, width), F32),
            pltpu.VMEM((share, width), F32),
            pltpu.VMEM((n_p, share, width), F32),
            pltpu.VMEM((count, width), F32),
            vec, vec, vec, vec,
            sem((6,)), sem((n,)), sem((n,)), sem((n_p,)), sem((n_p,)),
            sem((2,)), sem((2,)), sem((n_c,)), sem((n_c,)),
        ],
        compiler_params=pltpu.CompilerParams(
            collective_id=0, has_side_effects=True, vmem_limit_bytes=40 << 20
        ),
        name="solve",
    )(dense.reshape(n, share, width), camera, damp, diag_inverse, coupling, wh, wl, xh, xl, rh, rl)
    return own, everyone.reshape(n_c * count, width)


def shards(n_c, n_p, cam_jac, point_jac, residual, obs_cam, damp_exp, cam_step, diag_inverse, coupling):
    blocks, observers = obs_cam.shape
    total_blocks = cam_step.shape[0] * n_c
    pairs = observers // 2

    def by_pair(x):
        comps = x.shape[1]
        return x.reshape(blocks, comps, pairs, 128).transpose(1, 2, 0, 3).reshape(comps, pairs * blocks, 128)

    cj, pj, res = by_pair(cam_jac), by_pair(point_jac), by_pair(residual)
    order = obs_cam.reshape(blocks, pairs, 2).transpose(2, 1, 0).reshape(-1)
    cams = lax.iota(jnp.int32, total_blocks)
    pick = (order[:, None] == cams[None, :]).astype(BF16)
    pick_t = (cams[:, None] == order[None, :]).astype(BF16)
    dampings = jnp.exp2(damp_exp.astype(F32))
    wide = jnp.tile(dampings, (1, 6))
    maps = sweep_maps(diag_inverse, coupling)
    camera = cam_step
    cam_all = lax.all_gather(camera, "chain", axis=0, tiled=True)
    for iteration in range(ITERS):
        damp = wide[iteration][None]
        dense = eliminate(cam_all, pick, pick_t, cj, pj, res, damp[:, :128], True)
        camera, cam_all = solve(n_c, n_p, dense, camera, damp, diag_inverse, coupling, maps)
    out = eliminate(cam_all, pick, pick_t, cj, pj, res, wide[ITERS - 1][None, :128], False)
    return camera, out[:, :, :64].transpose(1, 0, 2)


def solution(mesh):
    in_specs = (
        P(("chain", "pts"), None, None),
        P(("chain", "pts"), None, None),
        P(("chain", "pts"), None, None),
        P(("chain", "pts"), None),
        P(),
        P("chain", None),
        P("chain", None, None),
        P("chain", None, None),
    )
    out_specs = (P("chain", None), P(("chain", "pts"), None, None))
    inner = functools.partial(shards, mesh.shape["chain"], mesh.shape["pts"])
    return jax.shard_map(inner, mesh=mesh, in_specs=in_specs, out_specs=out_specs, check_vma=False)
```

```python
import functools

import jax
import jax.numpy as jnp
from jax import lax
from jax.experimental import pallas as pl
from jax.experimental.pallas import tpu as pltpu
from jax.sharding import PartitionSpec as P

ITERS = 2
MESH = pl.DeviceIdType.MESH
F32, BF16 = jnp.float32, jnp.bfloat16
VMEM = pl.BlockSpec(memory_space=pltpu.VMEM)
ANY = pl.BlockSpec(memory_space=pl.ANY)


def dot_rows(x, panel):
    return lax.dot_general(x, panel, (((1,), (0,)), ((), ())), preferred_element_type=F32)


def dot_cols(x, panel):
    return lax.dot_general(x, panel, (((1,), (1,)), ((), ())), preferred_element_type=F32)


def halves(x):
    high = x.astype(BF16)
    return high, (x - high.astype(F32)).astype(BF16)


def thirds(x):
    high = x.astype(BF16)
    rest = x - high.astype(F32)
    mid = rest.astype(BF16)
    return high, mid, (rest - mid.astype(F32)).astype(BF16)


def eliminate(adjoint_out, cameras, pick_ref, pick_t_ref, cj_ref, pj_ref, res_ref, damp, out_ref, seen, parts):
    rows = res_ref.shape[1]
    blocks = rows // 4
    high, mid, low = thirds(cameras)
    pick = pick_ref[...]
    seen[...] = (dot_rows(pick, low) + dot_rows(pick, mid)) + dot_rows(pick, high)
    step = 16
    left = lax.broadcasted_iota(jnp.int32, (step, 128), 1) < 64

    def swap(x):
        return pltpu.roll(x, 64, 1)

    def chunk(i, carry):
        at = pl.multiple_of(i * step, step)
        misfits, points = [], []
        hess = [None] * 6
        target = [None] * 3
        pairs = ((0, 0), (0, 1), (0, 2), (1, 1), (1, 2), (2, 2))
        for tp in range(4):
            here = pl.ds(tp * blocks + at, step)
            there = pl.ds(rows + tp * blocks + at, step)
            cams = []
            for c in range(3):
                even = seen[here, c * 128 : (c + 1) * 128]
                odd = seen[there, c * 128 : (c + 1) * 128]
                cams.append(jnp.where(left, even, swap(odd)))
                cams.append(jnp.where(left, swap(even), odd))
            for a in range(2):
                miss = res_ref[a, here, :]
                for m in range(6):
                    miss = miss + cj_ref[6 * a + m, here, :].astype(F32) * cams[m]
                terms = [pj_ref[3 * a + n, here, :].astype(F32) for n in range(3)]
                misfits.append(miss)
                points.append(terms)
                for e, (n, k) in enumerate(pairs):
                    new = terms[n] * terms[k]
                    hess[e] = new if hess[e] is None else hess[e] + new
                for n in range(3):
                    new = terms[n] * miss
                    target[n] = new if target[n] is None else target[n] + new
        hess = [h + swap(h) for h in hess]
        ta, tb, tc = [t + swap(t) for t in target]
        aa, ab, ac, bb, bc, cc = hess
        aa, bb, cc = aa + damp, bb + damp, cc + damp
        cof_aa = bb * cc - bc * bc
        cof_ab = ac * bc - ab * cc
        cof_ac = ab * bc - ac * bb
        cof_bb = aa * cc - ac * ac
        cof_bc = ab * ac - aa * bc
        cof_cc = aa * bb - ab * ab
        det = aa * cof_aa + ab * cof_ab + ac * cof_ac
        sol = (
            (cof_aa * ta + cof_ab * tb + cof_ac * tc) / det,
            (cof_ab * ta + cof_bb * tb + cof_bc * tc) / det,
            (cof_ac * ta + cof_bc * tb + cof_cc * tc) / det,
        )
        if not adjoint_out:
            for n in range(3):
                out_ref[n, pl.ds(at, step), :] = -sol[n]
            return carry
        for tp in range(4):
            here = pl.ds(tp * blocks + at, step)
            there = pl.ds(rows + tp * blocks + at, step)
            left_over = []
            for a in range(2):
                terms = points[2 * tp + a]
                left_over.append(
                    misfits[2 * tp + a]
                    - (terms[0] * sol[0] + terms[1] * sol[1] + terms[2] * sol[2])
                )
            adj = [
                cj_ref[m, here, :].astype(F32) * left_over[0]
                + cj_ref[6 + m, here, :].astype(F32) * left_over[1]
                for m in range(6)
            ]
            for c in range(3):
                span = slice(c * 128, (c + 1) * 128)
                even = jnp.where(left, adj[2 * c], swap(adj[2 * c + 1]))
                odd = jnp.where(left, swap(adj[2 * c]), adj[2 * c + 1])
                for part, value in enumerate(thirds(even)):
                    parts[part, here, span] = value
                for part, value in enumerate(thirds(odd)):
                    parts[part, there, span] = value
        return carry

    lax.fori_loop(0, blocks // step, chunk, 0)
    if adjoint_out:
        pick_t = pick_t_ref[...]
        out_ref[...] = (
            dot_rows(pick_t, parts[2]) + dot_rows(pick_t, parts[1])
        ) + dot_rows(pick_t, parts[0])


def split_row(v):
    row = lax.broadcasted_iota(jnp.int32, v.shape, 0)
    high = v.astype(BF16).astype(F32)
    rest = v - high
    mid = rest.astype(BF16).astype(F32)
    low = rest - mid
    return jnp.where(row == 0, high, jnp.where(row == 1, mid, jnp.where(row == 2, low, 0.0))).astype(BF16)


def total(y):
    return jnp.broadcast_to(jnp.sum(y, axis=0, keepdims=True), y.shape)


def times(v, panel):
    return total(dot_rows(split_row(v), panel))


def times_t(v, panel):
    return total(dot_cols(split_row(v), panel))


def stacked(dot, x, panel):
    rows = x.shape[0]
    both = dot(jnp.concatenate(halves(x), axis=0), panel)
    return both[:rows] + both[rows:]


def whole_kernel(
    n_c, n_p,
    order_ref, cam_ref, damp_ref, cj_hbm, pj_hbm, res_hbm, d_hbm, c_hbm,
    cam_out, point_out,
    cj_ref, pj_ref, res_ref, d_ref, c_ref, wh_ref, wl_ref, xh_ref, xl_ref, rh_ref, rl_ref, run_f, run_b,
    pick, pick_t, seen, parts, dense, own, every,
    landed, piece, grad, solved, update, carry_in, carry_out,
    load_sem, rs_send, rs_recv, pts_send, pts_recv, ring_send, ring_recv, all_send, all_recv,
):
    me_c, me_p = lax.axis_index("chain"), lax.axis_index("pts")
    count, width = cam_ref.shape
    rows = res_ref.shape[1]
    loads = [
        pltpu.make_async_copy(src, dst, load_sem.at[i])
        for i, (src, dst) in enumerate(
            ((d_hbm, d_ref), (c_hbm, c_ref), (cj_hbm, cj_ref), (pj_hbm, pj_ref), (res_hbm, res_ref))
        )
    ]
    for load in loads:
        load.start()

    barrier = pltpu.get_barrier_semaphore()

    @pl.loop(1, n_c)
    def _(i):
        pl.semaphore_signal(
            barrier, inc=1, device_id=(lax.rem(me_c + i, n_c), me_p), device_id_type=MESH
        )

    for i in range(1, n_p):
        pl.semaphore_signal(
            barrier, inc=1, device_id=(me_c, lax.rem(me_p + i, n_p)), device_id_type=MESH
        )
    pl.semaphore_wait(barrier, n_c + n_p - 2)

    def all_copy(turn, i):
        return pltpu.make_async_remote_copy(
            src_ref=own.at[turn],
            dst_ref=every.at[turn, me_c],
            send_sem=all_send.at[turn, i],
            recv_sem=all_recv.at[turn, i],
            device_id=(lax.rem(me_c + i, n_c), me_p),
            device_id_type=MESH,
        )

    def share_camera(turn):
        @pl.loop(1, n_c)
        def _(i):
            all_copy(turn, i).start()

        every[turn, me_c] = own[turn]

    def await_cameras(turn):
        @pl.loop(1, n_c)
        def _(i):
            all_copy(turn, i).wait()

    own[0] = cam_ref[...]
    share_camera(0)

    cams = lax.broadcasted_iota(jnp.int32, pick_t.shape, 0)
    chosen = jnp.where(cams == jnp.broadcast_to(order_ref[...], pick_t.shape), 1.0, 0.0)
    pick_t[...] = chosen.astype(BF16)
    pick[...] = chosen.T.astype(BF16)

    unit = (
        lax.broadcasted_iota(jnp.int32, (width, width), 0)
        == lax.broadcasted_iota(jnp.int32, (width, width), 1)
    ).astype(F32)
    run_f[...] = unit
    run_b[...] = unit

    def map_step(k, carry):
        back = count - 1 - k
        made = -stacked(dot_rows, run_f[...], d_ref[k])
        high, low = halves(made)
        wh_ref[k] = high
        wl_ref[k] = low
        run_f[...] = stacked(dot_rows, made, c_ref[k])
        made = stacked(dot_cols, -stacked(dot_cols, run_b[...], c_ref[back]), d_ref[back])
        run_b[...] = made
        high, low = halves(made)
        xh_ref[back] = high
        xl_ref[back] = low
        return carry

    loads[0].wait()
    loads[1].wait()
    lax.fori_loop(0, 2, map_step, 0)
    for load in loads[2:]:
        load.wait()
    await_cameras(0)

    def zero_ahead():
        carried = None
        for k in range(count):
            g = jnp.broadcast_to(grad[k : k + 1, :], carry_in.shape[2:])
            s = times(g if carried is None else g - carried, d_ref[k])
            solved[k : k + 1, :] = s[0:1]
            if k < count - 1:
                carried = times(s, c_ref[k])

    def zero_back():
        later = None
        for k in reversed(range(count)):
            r = jnp.broadcast_to(solved[k : k + 1, :], carry_in.shape[2:])
            if later is not None:
                r = r - times_t(later, c_ref[k])
            later = times_t(r, d_ref[k])
            update[k : k + 1, :] = later[0:1]

    def reach(vectors, high_ref, low_ref):
        acc = None
        for k in range(count):
            x = split_row(jnp.broadcast_to(vectors[k : k + 1, :], carry_in.shape[2:]))
            new = dot_cols(x, high_ref[k]) + dot_cols(x, low_ref[k])
            acc = new if acc is None else acc + new
        return -total(acc)

    def correct(x, out, high_ref, low_ref):
        for k in range(count):
            y = dot_rows(x, high_ref[k]) + dot_rows(x, low_ref[k])
            out[k : k + 1, :] = out[k : k + 1, :] + jnp.sum(y, axis=0, keepdims=True)

    def inner_step(it, carry):
        damp = damp_ref[it]
        cameras = every[it].reshape(n_c * count, width)
        eliminate(True, cameras, pick, pick_t, cj_ref, pj_ref, res_ref, damp[:, :128], dense, seen, parts)

        def rs_copy(i):
            to = lax.rem(me_c + i, n_c)
            return pltpu.make_async_remote_copy(
                src_ref=dense.at[pl.ds(pl.multiple_of(to * count, count), count)],
                dst_ref=landed.at[it, i],
                send_sem=rs_send.at[it, i],
                recv_sem=rs_recv.at[it, i],
                device_id=(to, me_p),
                device_id_type=MESH,
            )

        @pl.loop(1, n_c)
        def _(i):
            rs_copy(i).start()

        landed[it, 0] = dense[pl.ds(pl.multiple_of(me_c * count, count), count), :]

        @pl.when(it == 0)
        def _():
            lax.fori_loop(2, count, map_step, 0)
            high, low = halves(run_f[...])
            rh_ref[...] = high
            rl_ref[...] = low

        @pl.loop(1, n_c)
        def _(i):
            rs_copy(i).wait()

        mine = jnp.sum(landed[it], axis=0)

        def pts_copy(i):
            return pltpu.make_async_remote_copy(
                src_ref=piece.at[it, me_p],
                dst_ref=piece.at[it, me_p],
                send_sem=pts_send.at[it, i],
                recv_sem=pts_recv.at[it, i],
                device_id=(me_c, lax.rem(me_p + i, n_p)),
                device_id_type=MESH,
            )

        piece[it, me_p] = mine
        for i in range(1, n_p):
            pts_copy(i).start()
        for i in range(1, n_p):
            pts_copy(i).wait()
        grad[...] = jnp.sum(piece[it], axis=0) + damp * own[it]

        def ring(way):
            to = lax.rem(me_c + (n_c - 1 if way else 1), n_c)
            return pltpu.make_async_remote_copy(
                src_ref=carry_out.at[it, way], dst_ref=carry_in.at[it, way],
                send_sem=ring_send.at[it, way], recv_sem=ring_recv.at[it, way],
                device_id=(to, me_p), device_id_type=MESH,
            )

        def pass_on(way, reached, map_high, map_low, sweep):
            turn = n_c - 1 - me_c if way else me_c

            @pl.when(turn >= 3)
            def _():
                sweep()

            @pl.when(turn == 0)
            def _():
                carry_in[it, way] = jnp.zeros(carry_in.shape[2:], F32)

            @pl.when(turn > 0)
            def _():
                ring(way).wait_recv()

            x = split_row(carry_in[it, way])
            carry_out[it, way] = reached + total(dot_rows(x, map_high) + dot_rows(x, map_low))

            @pl.when(turn < n_c - 1)
            def _():
                ring(way).start()

            @pl.when(turn < 3)
            def _():
                sweep()

            return x

        x = pass_on(0, reach(grad, xh_ref, xl_ref), rh_ref[...], rl_ref[...], zero_ahead)
        correct(x, solved, wh_ref, wl_ref)
        x = pass_on(1, reach(solved, wh_ref, wl_ref), xh_ref[0], xl_ref[0], zero_back)
        correct(x, update, xh_ref, xl_ref)
        own[it + 1] = own[it] - update[...]
        share_camera(it + 1)

        @pl.when(me_c < n_c - 1)
        def _():
            ring(0).wait_send()

        @pl.when(me_c > 0)
        def _():
            ring(1).wait_send()

        await_cameras(it + 1)
        return carry

    lax.fori_loop(0, ITERS, inner_step, 0)
    cam_out[...] = own[ITERS]
    cameras = every[ITERS].reshape(n_c * count, width)
    eliminate(
        False, cameras, pick, pick_t, cj_ref, pj_ref, res_ref, damp_ref[ITERS - 1][:, :128], point_out, seen, parts
    )


def shards(n_c, n_p, cam_jac, point_jac, residual, obs_cam, damp_exp, cam_step, diag_inverse, coupling):
    blocks, observers = obs_cam.shape
    count, width = cam_step.shape
    total_blocks = count * n_c
    pairs = observers // 2
    rows = pairs * blocks

    def by_pair(x):
        comps = x.shape[1]
        return x.reshape(blocks, comps, pairs, 128).transpose(1, 2, 0, 3).reshape(comps, rows, 128)

    cj, pj, res = by_pair(cam_jac), by_pair(point_jac), by_pair(residual)
    order = obs_cam.reshape(blocks, pairs, 2).transpose(2, 1, 0).reshape(1, -1)
    wide = jnp.tile(jnp.exp2(damp_exp.astype(F32)), (1, 6))[:, None, :]
    panel = pltpu.VMEM((count, width, width), BF16)
    square = (width, width)
    sem = pltpu.SemaphoreType.DMA
    camera, out = pl.pallas_call(
        functools.partial(whole_kernel, n_c, n_p),
        in_specs=[VMEM] * 3 + [ANY] * 5,
        out_specs=[VMEM, VMEM],
        out_shape=[
            jax.ShapeDtypeStruct((count, width), F32),
            jax.ShapeDtypeStruct((3, blocks, 128), F32),
        ],
        scratch_shapes=[pltpu.VMEM(x.shape, x.dtype) for x in (cj, pj, res)]
        + [panel] * 6
        + [pltpu.VMEM(square, BF16)] * 2
        + [pltpu.VMEM(square, F32)] * 2
        + [
            pltpu.VMEM((2 * rows, total_blocks), BF16),
            pltpu.VMEM((total_blocks, 2 * rows), BF16),
            pltpu.VMEM((2 * rows, width), F32),
            pltpu.VMEM((3, 2 * rows, width), BF16),
            pltpu.VMEM((total_blocks, width), F32),
            pltpu.VMEM((ITERS + 1, count, width), F32),
            pltpu.VMEM((ITERS + 1, n_c, count, width), F32),
            pltpu.VMEM((ITERS, n_c, count, width), F32),
            pltpu.VMEM((ITERS, n_p, count, width), F32),
            pltpu.VMEM((count, width), F32),
            pltpu.VMEM((count, width), F32),
            pltpu.VMEM((count, width), F32),
            pltpu.VMEM((ITERS, 2, 8, width), F32),
            pltpu.VMEM((ITERS, 2, 8, width), F32),
            sem((5,)), sem((ITERS, n_c)), sem((ITERS, n_c)), sem((ITERS, n_p)), sem((ITERS, n_p)),
            sem((ITERS, 2)), sem((ITERS, 2)), sem((ITERS + 1, n_c)), sem((ITERS + 1, n_c)),
        ],
        compiler_params=pltpu.CompilerParams(
            collective_id=0, has_side_effects=True, vmem_limit_bytes=48 << 20
        ),
        name="camera_steps",
    )(order, cam_step, wide, cj, pj, res, diag_inverse, coupling)
    return camera, out[:, :, :64].transpose(1, 0, 2)


def solution(mesh):
    in_specs = (
        P(("chain", "pts"), None, None),
        P(("chain", "pts"), None, None),
        P(("chain", "pts"), None, None),
        P(("chain", "pts"), None),
        P(),
        P("chain", None),
        P("chain", None, None),
        P("chain", None, None),
    )
    out_specs = (P("chain", None), P(("chain", "pts"), None, None))
    inner = functools.partial(shards, mesh.shape["chain"], mesh.shape["pts"])
    return jax.shard_map(inner, mesh=mesh, in_specs=in_specs, out_specs=out_specs, check_vma=False)
```

```python
import functools

import jax
import jax.numpy as jnp
from jax import lax
from jax.experimental import pallas as pl
from jax.experimental.pallas import tpu as pltpu
from jax.sharding import PartitionSpec as P

ITERS = 2
MESH = pl.DeviceIdType.MESH
F32, BF16 = jnp.float32, jnp.bfloat16
VMEM = pl.BlockSpec(memory_space=pltpu.VMEM)
ANY = pl.BlockSpec(memory_space=pl.ANY)


def dot_rows(x, panel):
    return lax.dot_general(x, panel, (((1,), (0,)), ((), ())), preferred_element_type=F32)


def dot_cols(x, panel):
    return lax.dot_general(x, panel, (((1,), (1,)), ((), ())), preferred_element_type=F32)


def halves(x):
    high = x.astype(BF16)
    return high, (x - high.astype(F32)).astype(BF16)


def thirds(x):
    high = x.astype(BF16)
    rest = x - high.astype(F32)
    mid = rest.astype(BF16)
    return high, mid, (rest - mid.astype(F32)).astype(BF16)


def eliminate(adjoint_out, cameras, pick_ref, pick_t_ref, cj_ref, pj_ref, res_ref, damp, out_ref, seen, parts):
    rows = res_ref.shape[1]
    blocks = rows // 4
    high, mid, low = thirds(cameras)
    pick = pick_ref[...]
    seen[...] = (dot_rows(pick, low) + dot_rows(pick, mid)) + dot_rows(pick, high)
    step = 16
    left = lax.broadcasted_iota(jnp.int32, (step, 128), 1) < 64

    def swap(x):
        return pltpu.roll(x, 64, 1)

    def chunk(i, carry):
        at = pl.multiple_of(i * step, step)
        misfits, points = [], []
        hess = [None] * 6
        target = [None] * 3
        pairs = ((0, 0), (0, 1), (0, 2), (1, 1), (1, 2), (2, 2))
        for tp in range(4):
            here = pl.ds(tp * blocks + at, step)
            there = pl.ds(rows + tp * blocks + at, step)
            cams = []
            for c in range(3):
                even = seen[here, c * 128 : (c + 1) * 128]
                odd = seen[there, c * 128 : (c + 1) * 128]
                cams.append(jnp.where(left, even, swap(odd)))
                cams.append(jnp.where(left, swap(even), odd))
            for a in range(2):
                miss = res_ref[a, here, :]
                for m in range(6):
                    miss = miss + cj_ref[6 * a + m, here, :].astype(F32) * cams[m]
                terms = [pj_ref[3 * a + n, here, :].astype(F32) for n in range(3)]
                misfits.append(miss)
                points.append(terms)
                for e, (n, k) in enumerate(pairs):
                    new = terms[n] * terms[k]
                    hess[e] = new if hess[e] is None else hess[e] + new
                for n in range(3):
                    new = terms[n] * miss
                    target[n] = new if target[n] is None else target[n] + new
        hess = [h + swap(h) for h in hess]
        ta, tb, tc = [t + swap(t) for t in target]
        aa, ab, ac, bb, bc, cc = hess
        aa, bb, cc = aa + damp, bb + damp, cc + damp
        cof_aa = bb * cc - bc * bc
        cof_ab = ac * bc - ab * cc
        cof_ac = ab * bc - ac * bb
        cof_bb = aa * cc - ac * ac
        cof_bc = ab * ac - aa * bc
        cof_cc = aa * bb - ab * ab
        det = aa * cof_aa + ab * cof_ab + ac * cof_ac
        sol = (
            (cof_aa * ta + cof_ab * tb + cof_ac * tc) / det,
            (cof_ab * ta + cof_bb * tb + cof_bc * tc) / det,
            (cof_ac * ta + cof_bc * tb + cof_cc * tc) / det,
        )
        if not adjoint_out:
            for n in range(3):
                out_ref[n, pl.ds(at, step), :] = -sol[n]
            return carry
        for tp in range(4):
            here = pl.ds(tp * blocks + at, step)
            there = pl.ds(rows + tp * blocks + at, step)
            left_over = []
            for a in range(2):
                terms = points[2 * tp + a]
                left_over.append(
                    misfits[2 * tp + a]
                    - (terms[0] * sol[0] + terms[1] * sol[1] + terms[2] * sol[2])
                )
            adj = [
                cj_ref[m, here, :].astype(F32) * left_over[0]
                + cj_ref[6 + m, here, :].astype(F32) * left_over[1]
                for m in range(6)
            ]
            for c in range(3):
                span = slice(c * 128, (c + 1) * 128)
                even = jnp.where(left, adj[2 * c], swap(adj[2 * c + 1]))
                odd = jnp.where(left, swap(adj[2 * c]), adj[2 * c + 1])
                for part, value in enumerate(thirds(even)):
                    parts[part, here, span] = value
                for part, value in enumerate(thirds(odd)):
                    parts[part, there, span] = value
        return carry

    lax.fori_loop(0, blocks // step, chunk, 0)
    if adjoint_out:
        pick_t = pick_t_ref[...]
        out_ref[...] = (
            dot_rows(pick_t, parts[2]) + dot_rows(pick_t, parts[1])
        ) + dot_rows(pick_t, parts[0])


def split_row(v):
    row = lax.broadcasted_iota(jnp.int32, v.shape, 0)
    high = v.astype(BF16).astype(F32)
    rest = v - high
    mid = rest.astype(BF16).astype(F32)
    low = rest - mid
    return jnp.where(row == 0, high, jnp.where(row == 1, mid, jnp.where(row == 2, low, 0.0))).astype(BF16)


def total(y):
    return jnp.broadcast_to(jnp.sum(y, axis=0, keepdims=True), y.shape)


def times(v, panel):
    return total(dot_rows(split_row(v), panel))


def times_t(v, panel):
    return total(dot_cols(split_row(v), panel))


def stacked(dot, x, panel):
    rows = x.shape[0]
    both = dot(jnp.concatenate(halves(x), axis=0), panel)
    return both[:rows] + both[rows:]


def whole_kernel(
    n_c, n_p,
    order_ref, cam_ref, damp_ref, cj_hbm, pj_hbm, res_hbm, d_hbm, c_hbm,
    cam_out, point_out,
    cj_ref, pj_ref, res_ref, d_ref, c_ref, wh_ref, wl_ref, xh_ref, xl_ref, rh_ref, rl_ref, run_f, run_b,
    pick, pick_t, seen, parts, dense, own, every,
    landed, piece, grad, solved, update, carry_in, carry_out, first_in, first_out, entry,
    run_nb, nh_ref, nl_ref, ph_ref, pk_ref,
    load_sem, rs_send, rs_recv, pts_send, pts_recv, ring_send, ring_recv, first_send, first_recv, all_send, all_recv, nb_send, nb_recv,
):
    me_c, me_p = lax.axis_index("chain"), lax.axis_index("pts")
    count, width = cam_ref.shape
    rows = res_ref.shape[1]
    loads = [
        pltpu.make_async_copy(src, dst, load_sem.at[i])
        for i, (src, dst) in enumerate(
            ((d_hbm, d_ref), (c_hbm, c_ref), (cj_hbm, cj_ref), (pj_hbm, pj_ref), (res_hbm, res_ref))
        )
    ]
    for load in loads:
        load.start()

    barrier = pltpu.get_barrier_semaphore()

    @pl.loop(1, n_c)
    def _(i):
        pl.semaphore_signal(
            barrier, inc=1, device_id=(lax.rem(me_c + i, n_c), me_p), device_id_type=MESH
        )

    for i in range(1, n_p):
        pl.semaphore_signal(
            barrier, inc=1, device_id=(me_c, lax.rem(me_p + i, n_p)), device_id_type=MESH
        )
    pl.semaphore_wait(barrier, n_c + n_p - 2)

    def all_copy(turn, i):
        return pltpu.make_async_remote_copy(
            src_ref=own.at[turn],
            dst_ref=every.at[turn, me_c],
            send_sem=all_send.at[turn, i],
            recv_sem=all_recv.at[turn, i],
            device_id=(lax.rem(me_c + i, n_c), me_p),
            device_id_type=MESH,
        )

    def share_camera(turn):
        @pl.loop(1, n_c)
        def _(i):
            all_copy(turn, i).start()

        every[turn, me_c] = own[turn]

    def await_cameras(turn):
        @pl.loop(1, n_c)
        def _(i):
            all_copy(turn, i).wait()

    own[0] = cam_ref[...]
    share_camera(0)

    cams = lax.broadcasted_iota(jnp.int32, pick_t.shape, 0)
    chosen = jnp.where(cams == jnp.broadcast_to(order_ref[...], pick_t.shape), 1.0, 0.0)
    pick_t[...] = chosen.astype(BF16)
    pick[...] = chosen.T.astype(BF16)

    unit = (
        lax.broadcasted_iota(jnp.int32, (width, width), 0)
        == lax.broadcasted_iota(jnp.int32, (width, width), 1)
    ).astype(F32)
    run_f[...] = unit
    run_b[...] = unit

    def map_ahead(k, carry):
        made = -stacked(dot_rows, run_f[...], d_ref[k])
        high, low = halves(made)
        wh_ref[k] = high
        wl_ref[k] = low
        run_f[...] = stacked(dot_rows, made, c_ref[k])
        return carry

    def map_back(i, carry):
        k = count - 1 - i
        made = stacked(dot_cols, -stacked(dot_cols, run_b[...], c_ref[k]), d_ref[k])
        run_b[...] = made
        high, low = halves(made)
        xh_ref[k] = high
        xl_ref[k] = low
        return carry

    odd = lax.rem(me_c, 2)
    swap_maps = pltpu.make_async_remote_copy(
        src_ref=run_f, dst_ref=run_nb, send_sem=nb_send, recv_sem=nb_recv,
        device_id=(me_c + 1 - 2 * odd, me_p), device_id_type=MESH,
    )

    def pair_map():
        high, low = halves(run_f[...])
        rh_ref[...] = high
        rl_ref[...] = low
        swap_maps.wait()
        mine, other = run_f[...], run_nb[...]
        nh_ref[...], nl_ref[...] = halves(other)
        early = jnp.where(odd == 1, other, mine)
        late_high, late_low = halves(jnp.where(odd == 1, mine, other))
        high, low = halves(stacked(dot_rows, early, late_high) + stacked(dot_rows, early, late_low))
        ph_ref[...] = high
        pk_ref[...] = low

    loads[0].wait()
    loads[1].wait()
    lax.fori_loop(0, 4, map_ahead, 0)
    for load in loads[2:]:
        load.wait()
    await_cameras(0)

    def zero_ahead():
        carried = None
        for k in range(count):
            g = jnp.broadcast_to(grad[k : k + 1, :], carry_in.shape[2:])
            s = times(g if carried is None else g - carried, d_ref[k])
            solved[k : k + 1, :] = s[0:1]
            if k < count - 1:
                carried = times(s, c_ref[k])

    def zero_back():
        later = None
        for k in reversed(range(count)):
            r = jnp.broadcast_to(solved[k : k + 1, :], carry_in.shape[2:])
            if later is not None:
                r = r - times_t(later, c_ref[k])
            later = times_t(r, d_ref[k])
            update[k : k + 1, :] = later[0:1]

    def reach(vectors, high_ref, low_ref):
        acc = None
        for k in range(count):
            x = split_row(jnp.broadcast_to(vectors[k : k + 1, :], carry_in.shape[2:]))
            new = dot_cols(x, high_ref[k]) + dot_cols(x, low_ref[k])
            acc = new if acc is None else acc + new
        return -total(acc)

    def correct(x, out, high_ref, low_ref):
        for k in range(count):
            y = dot_rows(x, high_ref[k]) + dot_rows(x, low_ref[k])
            out[k : k + 1, :] = out[k : k + 1, :] + jnp.sum(y, axis=0, keepdims=True)

    def inner_step(it, carry):
        damp = damp_ref[it]
        cameras = every[it].reshape(n_c * count, width)
        eliminate(True, cameras, pick, pick_t, cj_ref, pj_ref, res_ref, damp[:, :128], dense, seen, parts)

        def rs_copy(i):
            to = lax.rem(me_c + i, n_c)
            return pltpu.make_async_remote_copy(
                src_ref=dense.at[pl.ds(pl.multiple_of(to * count, count), count)],
                dst_ref=landed.at[it, i],
                send_sem=rs_send.at[it, i],
                recv_sem=rs_recv.at[it, i],
                device_id=(to, me_p),
                device_id_type=MESH,
            )

        @pl.loop(1, n_c)
        def _(i):
            rs_copy(i).start()

        landed[it, 0] = dense[pl.ds(pl.multiple_of(me_c * count, count), count), :]

        @pl.when(it == 0)
        def _():
            lax.fori_loop(4, count, map_ahead, 0)
            swap_maps.start()
            lax.fori_loop(0, count, map_back, 0)
            pair_map()

        @pl.loop(1, n_c)
        def _(i):
            rs_copy(i).wait()

        mine = jnp.sum(landed[it], axis=0)

        def pts_copy(i):
            return pltpu.make_async_remote_copy(
                src_ref=piece.at[it, me_p],
                dst_ref=piece.at[it, me_p],
                send_sem=pts_send.at[it, i],
                recv_sem=pts_recv.at[it, i],
                device_id=(me_c, lax.rem(me_p + i, n_p)),
                device_id_type=MESH,
            )

        piece[it, me_p] = mine
        for i in range(1, n_p):
            pts_copy(i).start()
        for i in range(1, n_p):
            pts_copy(i).wait()
        grad[...] = jnp.sum(piece[it], axis=0) + damp * own[it]

        def hand(way):
            return pltpu.make_async_remote_copy(
                src_ref=first_out.at[it, way], dst_ref=first_in.at[it, way],
                send_sem=first_send.at[it, way], recv_sem=first_recv.at[it, way],
                device_id=(me_c + 1 - 2 * odd, me_p), device_id_type=MESH,
            )

        def ring(way, far):
            to = lax.rem(me_c + (n_c - far if way else far), n_c)
            return pltpu.make_async_remote_copy(
                src_ref=carry_out.at[it, way], dst_ref=carry_in.at[it, way],
                send_sem=ring_send.at[it, way, far - 1], recv_sem=ring_recv.at[it, way],
                device_id=(to, me_p), device_id_type=MESH,
            )

        def seat(way):
            turn = n_c - 1 - me_c if way else me_c
            return lax.rem(turn, 2) == 1, turn // 2

        def pass_on(way, reached, map_high, map_low, sweep):
            second, group = seat(way)
            dot = dot_cols if way else dot_rows

            def arrive():
                @pl.when(group == 0)
                def _():
                    carry_in[it, way] = jnp.zeros(carry_in.shape[2:], F32)

                @pl.when(group > 0)
                def _():
                    ring(way, 2).wait_recv()

                return carry_in[it, way]

            first_out[it, way] = reached

            @pl.when(jnp.logical_not(second))
            def _():
                hand(way).start()
                sweep()
                entry[...] = arrive()

            @pl.when(second)
            def _():
                @pl.when(group >= 2)
                def _():
                    sweep()

                hand(way).wait_recv()
                given = first_in[it, way]
                x = split_row(given)
                both = first_out[it, way] + total(dot_rows(x, map_high[...]) + dot_rows(x, map_low[...]))
                x = split_row(arrive())
                carry_out[it, way] = both + total(dot(x, ph_ref[...]) + dot(x, pk_ref[...]))

                @pl.when(group < n_c // 2 - 1)
                def _():
                    ring(way, 2).start()
                    ring(way, 1).start()

                entry[...] = given + total(dot(x, nh_ref[...]) + dot(x, nl_ref[...]))

                @pl.when(group < 2)
                def _():
                    sweep()

            return split_row(entry[...])

        def drain(way):
            second, group = seat(way)

            @pl.when(jnp.logical_not(second))
            def _():
                hand(way).wait_send()

            @pl.when(jnp.logical_and(second, group < n_c // 2 - 1))
            def _():
                ring(way, 2).wait_send()
                ring(way, 1).wait_send()

        x = pass_on(0, reach(grad, xh_ref, xl_ref), rh_ref, rl_ref, zero_ahead)
        correct(x, solved, wh_ref, wl_ref)
        x = pass_on(1, reach(solved, wh_ref, wl_ref), xh_ref.at[0], xl_ref.at[0], zero_back)
        correct(x, update, xh_ref, xl_ref)
        own[it + 1] = own[it] - update[...]
        share_camera(it + 1)

        drain(0)
        drain(1)
        await_cameras(it + 1)
        return carry

    lax.fori_loop(0, ITERS, inner_step, 0)
    cam_out[...] = own[ITERS]
    cameras = every[ITERS].reshape(n_c * count, width)
    eliminate(
        False, cameras, pick, pick_t, cj_ref, pj_ref, res_ref, damp_ref[ITERS - 1][:, :128], point_out, seen, parts
    )


def shards(n_c, n_p, cam_jac, point_jac, residual, obs_cam, damp_exp, cam_step, diag_inverse, coupling):
    blocks, observers = obs_cam.shape
    count, width = cam_step.shape
    total_blocks = count * n_c
    pairs = observers // 2
    rows = pairs * blocks

    def by_pair(x):
        comps = x.shape[1]
        return x.reshape(blocks, comps, pairs, 128).transpose(1, 2, 0, 3).reshape(comps, rows, 128)

    cj, pj, res = by_pair(cam_jac), by_pair(point_jac), by_pair(residual)
    order = obs_cam.reshape(blocks, pairs, 2).transpose(2, 1, 0).reshape(1, -1)
    wide = jnp.tile(jnp.exp2(damp_exp.astype(F32)), (1, 6))[:, None, :]
    panel = pltpu.VMEM((count, width, width), BF16)
    square = (width, width)
    sem = pltpu.SemaphoreType.DMA
    camera, out = pl.pallas_call(
        functools.partial(whole_kernel, n_c, n_p),
        in_specs=[VMEM] * 3 + [ANY] * 5,
        out_specs=[VMEM, VMEM],
        out_shape=[
            jax.ShapeDtypeStruct((count, width), F32),
            jax.ShapeDtypeStruct((3, blocks, 128), F32),
        ],
        scratch_shapes=[pltpu.VMEM(x.shape, x.dtype) for x in (cj, pj, res)]
        + [panel] * 6
        + [pltpu.VMEM(square, BF16)] * 2
        + [pltpu.VMEM(square, F32)] * 2
        + [
            pltpu.VMEM((2 * rows, total_blocks), BF16),
            pltpu.VMEM((total_blocks, 2 * rows), BF16),
            pltpu.VMEM((2 * rows, width), F32),
            pltpu.VMEM((3, 2 * rows, width), BF16),
            pltpu.VMEM((total_blocks, width), F32),
            pltpu.VMEM((ITERS + 1, count, width), F32),
            pltpu.VMEM((ITERS + 1, n_c, count, width), F32),
            pltpu.VMEM((ITERS, n_c, count, width), F32),
            pltpu.VMEM((ITERS, n_p, count, width), F32),
            pltpu.VMEM((count, width), F32),
            pltpu.VMEM((count, width), F32),
            pltpu.VMEM((count, width), F32),
            pltpu.VMEM((ITERS, 2, 8, width), F32),
            pltpu.VMEM((ITERS, 2, 8, width), F32),
            pltpu.VMEM((ITERS, 2, 8, width), F32),
            pltpu.VMEM((ITERS, 2, 8, width), F32),
            pltpu.VMEM((8, width), F32),
            pltpu.VMEM(square, F32),
            pltpu.VMEM(square, BF16),
            pltpu.VMEM(square, BF16),
            pltpu.VMEM(square, BF16),
            pltpu.VMEM(square, BF16),
            sem((5,)), sem((ITERS, n_c)), sem((ITERS, n_c)), sem((ITERS, n_p)), sem((ITERS, n_p)),
            sem((ITERS, 2, 2)), sem((ITERS, 2)), sem((ITERS, 2)), sem((ITERS, 2)),
            sem((ITERS + 1, n_c)), sem((ITERS + 1, n_c)), sem(()), sem(()),
        ],
        compiler_params=pltpu.CompilerParams(
            collective_id=0, has_side_effects=True, vmem_limit_bytes=48 << 20
        ),
        name="camera_steps",
    )(order, cam_step, wide, cj, pj, res, diag_inverse, coupling)
    return camera, out[:, :, :64].transpose(1, 0, 2)


def solution(mesh):
    in_specs = (
        P(("chain", "pts"), None, None),
        P(("chain", "pts"), None, None),
        P(("chain", "pts"), None, None),
        P(("chain", "pts"), None),
        P(),
        P("chain", None),
        P("chain", None, None),
        P("chain", None, None),
    )
    out_specs = (P("chain", None), P(("chain", "pts"), None, None))
    inner = functools.partial(shards, mesh.shape["chain"], mesh.shape["pts"])
    return jax.shard_map(inner, mesh=mesh, in_specs=in_specs, out_specs=out_specs, check_vma=False)
```

```python
import functools

import jax
import jax.numpy as jnp
from jax import lax
from jax.experimental import pallas as pl
from jax.experimental.pallas import tpu as pltpu
from jax.sharding import PartitionSpec as P

ITERS = 2
MESH = pl.DeviceIdType.MESH
F32, BF16 = jnp.float32, jnp.bfloat16
VMEM = pl.BlockSpec(memory_space=pltpu.VMEM)
ANY = pl.BlockSpec(memory_space=pl.ANY)


def dot_rows(x, panel):
    return lax.dot_general(x, panel, (((1,), (0,)), ((), ())), preferred_element_type=F32)


def dot_cols(x, panel):
    return lax.dot_general(x, panel, (((1,), (1,)), ((), ())), preferred_element_type=F32)


def halves(x):
    high = x.astype(BF16)
    return high, (x - high.astype(F32)).astype(BF16)


def thirds(x):
    high = x.astype(BF16)
    rest = x - high.astype(F32)
    mid = rest.astype(BF16)
    return high, mid, (rest - mid.astype(F32)).astype(BF16)


def eliminate(adjoint_out, cameras, pick_ref, pick_t_ref, cj_ref, pj_ref, res_ref, damp, out_ref, seen, parts):
    rows = res_ref.shape[1]
    blocks = rows // 4
    high, mid, low = thirds(cameras)
    pick = pick_ref[...]
    seen[...] = (dot_rows(pick, low) + dot_rows(pick, mid)) + dot_rows(pick, high)
    step = 16
    left = lax.broadcasted_iota(jnp.int32, (step, 128), 1) < 64

    def swap(x):
        return pltpu.roll(x, 64, 1)

    def chunk(i, carry):
        at = pl.multiple_of(i * step, step)
        misfits, points = [], []
        hess = [None] * 6
        target = [None] * 3
        pairs = ((0, 0), (0, 1), (0, 2), (1, 1), (1, 2), (2, 2))
        for tp in range(4):
            here = pl.ds(tp * blocks + at, step)
            there = pl.ds(rows + tp * blocks + at, step)
            cams = []
            for c in range(3):
                even = seen[here, c * 128 : (c + 1) * 128]
                odd = seen[there, c * 128 : (c + 1) * 128]
                cams.append(jnp.where(left, even, swap(odd)))
                cams.append(jnp.where(left, swap(even), odd))
            for a in range(2):
                miss = res_ref[a, here, :]
                for m in range(6):
                    miss = miss + cj_ref[6 * a + m, here, :].astype(F32) * cams[m]
                terms = [pj_ref[3 * a + n, here, :].astype(F32) for n in range(3)]
                misfits.append(miss)
                points.append(terms)
                for e, (n, k) in enumerate(pairs):
                    new = terms[n] * terms[k]
                    hess[e] = new if hess[e] is None else hess[e] + new
                for n in range(3):
                    new = terms[n] * miss
                    target[n] = new if target[n] is None else target[n] + new
        hess = [h + swap(h) for h in hess]
        ta, tb, tc = [t + swap(t) for t in target]
        aa, ab, ac, bb, bc, cc = hess
        aa, bb, cc = aa + damp, bb + damp, cc + damp
        cof_aa = bb * cc - bc * bc
        cof_ab = ac * bc - ab * cc
        cof_ac = ab * bc - ac * bb
        cof_bb = aa * cc - ac * ac
        cof_bc = ab * ac - aa * bc
        cof_cc = aa * bb - ab * ab
        det = aa * cof_aa + ab * cof_ab + ac * cof_ac
        sol = (
            (cof_aa * ta + cof_ab * tb + cof_ac * tc) / det,
            (cof_ab * ta + cof_bb * tb + cof_bc * tc) / det,
            (cof_ac * ta + cof_bc * tb + cof_cc * tc) / det,
        )
        if not adjoint_out:
            for n in range(3):
                out_ref[n, pl.ds(at, step), :] = -sol[n]
            return carry
        for tp in range(4):
            here = pl.ds(tp * blocks + at, step)
            there = pl.ds(rows + tp * blocks + at, step)
            left_over = []
            for a in range(2):
                terms = points[2 * tp + a]
                left_over.append(
                    misfits[2 * tp + a]
                    - (terms[0] * sol[0] + terms[1] * sol[1] + terms[2] * sol[2])
                )
            adj = [
                cj_ref[m, here, :].astype(F32) * left_over[0]
                + cj_ref[6 + m, here, :].astype(F32) * left_over[1]
                for m in range(6)
            ]
            for c in range(3):
                span = slice(c * 128, (c + 1) * 128)
                even = jnp.where(left, adj[2 * c], swap(adj[2 * c + 1]))
                odd = jnp.where(left, swap(adj[2 * c]), adj[2 * c + 1])
                for part, value in enumerate(thirds(even)):
                    parts[part, here, span] = value
                for part, value in enumerate(thirds(odd)):
                    parts[part, there, span] = value
        return carry

    lax.fori_loop(0, blocks // step, chunk, 0)
    if adjoint_out:
        pick_t = pick_t_ref[...]
        out_ref[...] = (
            dot_rows(pick_t, parts[2]) + dot_rows(pick_t, parts[1])
        ) + dot_rows(pick_t, parts[0])


def split_row(v):
    row = lax.broadcasted_iota(jnp.int32, v.shape, 0)
    high = v.astype(BF16).astype(F32)
    rest = v - high
    mid = rest.astype(BF16).astype(F32)
    low = rest - mid
    return jnp.where(row == 0, high, jnp.where(row == 1, mid, jnp.where(row == 2, low, 0.0))).astype(BF16)


def total(y):
    return jnp.broadcast_to(jnp.sum(y, axis=0, keepdims=True), y.shape)


def times(v, panel):
    return total(dot_rows(split_row(v), panel))


def times_t(v, panel):
    return total(dot_cols(split_row(v), panel))


def stacked(dot, x, panel):
    rows = x.shape[0]
    both = dot(jnp.concatenate(halves(x), axis=0), panel)
    return both[:rows] + both[rows:]


def whole_kernel(
    n_c, n_p,
    order_ref, cam_ref, damp_ref, cj_hbm, pj_hbm, res_hbm, d_hbm, c_hbm,
    cam_out, point_out,
    cj_ref, pj_ref, res_ref, d_ref, c_ref, wh_ref, wl_ref, xh_ref, xl_ref, rh_ref, rl_ref, run_f, run_b,
    pick, pick_t, seen, parts, dense, own, every,
    landed, piece, grad, solved, update, carry_in, carry_out, first_in, first_out, entry,
    run_nb, nh_ref, nl_ref, ph_ref, pk_ref,
    load_sem, rs_send, rs_recv, pts_send, pts_recv, ring_send, ring_recv, first_send, first_recv, all_send, all_recv, nb_send, nb_recv,
):
    me_c, me_p = lax.axis_index("chain"), lax.axis_index("pts")
    count, width = cam_ref.shape
    rows = res_ref.shape[1]
    loads = [
        pltpu.make_async_copy(src, dst, load_sem.at[i])
        for i, (src, dst) in enumerate(
            ((d_hbm, d_ref), (c_hbm, c_ref), (cj_hbm, cj_ref), (pj_hbm, pj_ref), (res_hbm, res_ref))
        )
    ]
    for load in loads:
        load.start()

    barrier = pltpu.get_barrier_semaphore()

    @pl.loop(1, n_c)
    def _(i):
        pl.semaphore_signal(
            barrier, inc=1, device_id=(lax.rem(me_c + i, n_c), me_p), device_id_type=MESH
        )

    for i in range(1, n_p):
        pl.semaphore_signal(
            barrier, inc=1, device_id=(me_c, lax.rem(me_p + i, n_p)), device_id_type=MESH
        )
    pl.semaphore_wait(barrier, n_c + n_p - 2)

    def all_copy(turn, i):
        return pltpu.make_async_remote_copy(
            src_ref=own.at[turn],
            dst_ref=every.at[turn, me_c],
            send_sem=all_send.at[turn, i],
            recv_sem=all_recv.at[turn, i],
            device_id=(lax.rem(me_c + i, n_c), me_p),
            device_id_type=MESH,
        )

    def share_camera(turn):
        @pl.loop(1, n_c)
        def _(i):
            all_copy(turn, i).start()

        every[turn, me_c] = own[turn]

    def await_cameras(turn):
        @pl.loop(1, n_c)
        def _(i):
            all_copy(turn, i).wait()

    own[0] = cam_ref[...]
    share_camera(0)

    cams = lax.broadcasted_iota(jnp.int32, pick_t.shape, 0)
    chosen = jnp.where(cams == jnp.broadcast_to(order_ref[...], pick_t.shape), 1.0, 0.0)
    pick_t[...] = chosen.astype(BF16)
    pick[...] = chosen.T.astype(BF16)

    unit = (
        lax.broadcasted_iota(jnp.int32, (width, width), 0)
        == lax.broadcasted_iota(jnp.int32, (width, width), 1)
    ).astype(F32)
    run_f[...] = unit
    run_b[...] = unit

    def map_ahead(k, carry):
        made = -stacked(dot_rows, run_f[...], d_ref[k])
        high, low = halves(made)
        wh_ref[k] = high
        wl_ref[k] = low
        run_f[...] = stacked(dot_rows, made, c_ref[k])
        return carry

    def map_back(i, carry):
        k = count - 1 - i
        made = stacked(dot_cols, -stacked(dot_cols, run_b[...], c_ref[k]), d_ref[k])
        run_b[...] = made
        high, low = halves(made)
        xh_ref[k] = high
        xl_ref[k] = low
        return carry

    odd = lax.rem(me_c, 2)
    swap_maps = pltpu.make_async_remote_copy(
        src_ref=run_f, dst_ref=run_nb, send_sem=nb_send, recv_sem=nb_recv,
        device_id=(me_c + 1 - 2 * odd, me_p), device_id_type=MESH,
    )

    def pair_map():
        high, low = halves(run_f[...])
        rh_ref[...] = high
        rl_ref[...] = low
        swap_maps.wait()
        mine, other = run_f[...], run_nb[...]
        nh_ref[...], nl_ref[...] = halves(other)
        early = jnp.where(odd == 1, other, mine)
        late_high, late_low = halves(jnp.where(odd == 1, mine, other))
        high, low = halves(stacked(dot_rows, early, late_high) + stacked(dot_rows, early, late_low))
        ph_ref[...] = high
        pk_ref[...] = low

    loads[0].wait()
    loads[1].wait()
    lax.fori_loop(0, count, map_ahead, 0)
    swap_maps.start()
    for load in loads[2:]:
        load.wait()
    await_cameras(0)

    def zero_ahead():
        carried = None
        for k in range(count):
            g = jnp.broadcast_to(grad[k : k + 1, :], carry_in.shape[2:])
            s = times(g if carried is None else g - carried, d_ref[k])
            solved[k : k + 1, :] = s[0:1]
            if k < count - 1:
                carried = times(s, c_ref[k])

    def zero_back():
        later = None
        for k in reversed(range(count)):
            r = jnp.broadcast_to(solved[k : k + 1, :], carry_in.shape[2:])
            if later is not None:
                r = r - times_t(later, c_ref[k])
            later = times_t(r, d_ref[k])
            update[k : k + 1, :] = later[0:1]

    def reach(vectors, high_ref, low_ref):
        acc = None
        for k in range(count):
            x = split_row(jnp.broadcast_to(vectors[k : k + 1, :], carry_in.shape[2:]))
            new = dot_cols(x, high_ref[k]) + dot_cols(x, low_ref[k])
            acc = new if acc is None else acc + new
        return -total(acc)

    def correct(x, out, high_ref, low_ref):
        for k in range(count):
            y = dot_rows(x, high_ref[k]) + dot_rows(x, low_ref[k])
            out[k : k + 1, :] = out[k : k + 1, :] + jnp.sum(y, axis=0, keepdims=True)

    def inner_step(it, carry):
        damp = damp_ref[it]
        cameras = every[it].reshape(n_c * count, width)
        eliminate(True, cameras, pick, pick_t, cj_ref, pj_ref, res_ref, damp[:, :128], dense, seen, parts)

        def rs_copy(i):
            to = lax.rem(me_c + i, n_c)
            return pltpu.make_async_remote_copy(
                src_ref=dense.at[pl.ds(pl.multiple_of(to * count, count), count)],
                dst_ref=landed.at[it, i],
                send_sem=rs_send.at[it, i],
                recv_sem=rs_recv.at[it, i],
                device_id=(to, me_p),
                device_id_type=MESH,
            )

        @pl.loop(1, n_c)
        def _(i):
            rs_copy(i).start()

        landed[it, 0] = dense[pl.ds(pl.multiple_of(me_c * count, count), count), :]

        @pl.when(it == 0)
        def _():
            lax.fori_loop(0, count, map_back, 0)

        @pl.loop(1, n_c)
        def _(i):
            rs_copy(i).wait()

        mine = jnp.sum(landed[it], axis=0)

        def pts_copy(i):
            return pltpu.make_async_remote_copy(
                src_ref=piece.at[it, me_p],
                dst_ref=piece.at[it, me_p],
                send_sem=pts_send.at[it, i],
                recv_sem=pts_recv.at[it, i],
                device_id=(me_c, lax.rem(me_p + i, n_p)),
                device_id_type=MESH,
            )

        piece[it, me_p] = mine
        for i in range(1, n_p):
            pts_copy(i).start()

        @pl.when(it == 0)
        def _():
            pair_map()

        for i in range(1, n_p):
            pts_copy(i).wait()
        grad[...] = jnp.sum(piece[it], axis=0) + damp * own[it]

        def hand(way):
            return pltpu.make_async_remote_copy(
                src_ref=first_out.at[it, way], dst_ref=first_in.at[it, way],
                send_sem=first_send.at[it, way], recv_sem=first_recv.at[it, way],
                device_id=(me_c + 1 - 2 * odd, me_p), device_id_type=MESH,
            )

        def ring(way, far):
            to = lax.rem(me_c + (n_c - far if way else far), n_c)
            return pltpu.make_async_remote_copy(
                src_ref=carry_out.at[it, way], dst_ref=carry_in.at[it, way],
                send_sem=ring_send.at[it, way, far - 1], recv_sem=ring_recv.at[it, way],
                device_id=(to, me_p), device_id_type=MESH,
            )

        def seat(way):
            turn = n_c - 1 - me_c if way else me_c
            return lax.rem(turn, 2) == 1, turn // 2

        def pass_on(way, reached, map_high, map_low, sweep):
            second, group = seat(way)
            dot = dot_cols if way else dot_rows

            def arrive():
                @pl.when(group == 0)
                def _():
                    carry_in[it, way] = jnp.zeros(carry_in.shape[2:], F32)

                @pl.when(group > 0)
                def _():
                    ring(way, 2).wait_recv()

                return carry_in[it, way]

            first_out[it, way] = reached

            @pl.when(jnp.logical_not(second))
            def _():
                hand(way).start()
                sweep()
                entry[...] = arrive()

            @pl.when(second)
            def _():
                @pl.when(group >= 2)
                def _():
                    sweep()

                hand(way).wait_recv()
                given = first_in[it, way]
                x = split_row(given)
                both = first_out[it, way] + total(dot_rows(x, map_high[...]) + dot_rows(x, map_low[...]))
                x = split_row(arrive())
                carry_out[it, way] = both + total(dot(x, ph_ref[...]) + dot(x, pk_ref[...]))

                @pl.when(group < n_c // 2 - 1)
                def _():
                    ring(way, 2).start()
                    ring(way, 1).start()

                entry[...] = given + total(dot(x, nh_ref[...]) + dot(x, nl_ref[...]))

                @pl.when(group < 2)
                def _():
                    sweep()

            return split_row(entry[...])

        def drain(way):
            second, group = seat(way)

            @pl.when(jnp.logical_not(second))
            def _():
                hand(way).wait_send()

            @pl.when(jnp.logical_and(second, group < n_c // 2 - 1))
            def _():
                ring(way, 2).wait_send()
                ring(way, 1).wait_send()

        x = pass_on(0, reach(grad, xh_ref, xl_ref), rh_ref, rl_ref, zero_ahead)
        correct(x, solved, wh_ref, wl_ref)
        x = pass_on(1, reach(solved, wh_ref, wl_ref), xh_ref.at[0], xl_ref.at[0], zero_back)
        correct(x, update, xh_ref, xl_ref)
        own[it + 1] = own[it] - update[...]
        share_camera(it + 1)

        drain(0)
        drain(1)
        await_cameras(it + 1)
        return carry

    lax.fori_loop(0, ITERS, inner_step, 0)
    cam_out[...] = own[ITERS]
    cameras = every[ITERS].reshape(n_c * count, width)
    eliminate(
        False, cameras, pick, pick_t, cj_ref, pj_ref, res_ref, damp_ref[ITERS - 1][:, :128], point_out, seen, parts
    )


def shards(n_c, n_p, cam_jac, point_jac, residual, obs_cam, damp_exp, cam_step, diag_inverse, coupling):
    blocks, observers = obs_cam.shape
    count, width = cam_step.shape
    total_blocks = count * n_c
    pairs = observers // 2
    rows = pairs * blocks

    def by_pair(x):
        comps = x.shape[1]
        return x.reshape(blocks, comps, pairs, 128).transpose(1, 2, 0, 3).reshape(comps, rows, 128)

    cj, pj, res = by_pair(cam_jac), by_pair(point_jac), by_pair(residual)
    order = obs_cam.reshape(blocks, pairs, 2).transpose(2, 1, 0).reshape(1, -1)
    wide = jnp.tile(jnp.exp2(damp_exp.astype(F32)), (1, 6))[:, None, :]
    panel = pltpu.VMEM((count, width, width), BF16)
    square = (width, width)
    sem = pltpu.SemaphoreType.DMA
    camera, out = pl.pallas_call(
        functools.partial(whole_kernel, n_c, n_p),
        in_specs=[VMEM] * 3 + [ANY] * 5,
        out_specs=[VMEM, VMEM],
        out_shape=[
            jax.ShapeDtypeStruct((count, width), F32),
            jax.ShapeDtypeStruct((3, blocks, 128), F32),
        ],
        scratch_shapes=[pltpu.VMEM(x.shape, x.dtype) for x in (cj, pj, res)]
        + [panel] * 6
        + [pltpu.VMEM(square, BF16)] * 2
        + [pltpu.VMEM(square, F32)] * 2
        + [
            pltpu.VMEM((2 * rows, total_blocks), BF16),
            pltpu.VMEM((total_blocks, 2 * rows), BF16),
            pltpu.VMEM((2 * rows, width), F32),
            pltpu.VMEM((3, 2 * rows, width), BF16),
            pltpu.VMEM((total_blocks, width), F32),
            pltpu.VMEM((ITERS + 1, count, width), F32),
            pltpu.VMEM((ITERS + 1, n_c, count, width), F32),
            pltpu.VMEM((ITERS, n_c, count, width), F32),
            pltpu.VMEM((ITERS, n_p, count, width), F32),
            pltpu.VMEM((count, width), F32),
            pltpu.VMEM((count, width), F32),
            pltpu.VMEM((count, width), F32),
            pltpu.VMEM((ITERS, 2, 8, width), F32),
            pltpu.VMEM((ITERS, 2, 8, width), F32),
            pltpu.VMEM((ITERS, 2, 8, width), F32),
            pltpu.VMEM((ITERS, 2, 8, width), F32),
            pltpu.VMEM((8, width), F32),
            pltpu.VMEM(square, F32),
            pltpu.VMEM(square, BF16),
            pltpu.VMEM(square, BF16),
            pltpu.VMEM(square, BF16),
            pltpu.VMEM(square, BF16),
            sem((5,)), sem((ITERS, n_c)), sem((ITERS, n_c)), sem((ITERS, n_p)), sem((ITERS, n_p)),
            sem((ITERS, 2, 2)), sem((ITERS, 2)), sem((ITERS, 2)), sem((ITERS, 2)),
            sem((ITERS + 1, n_c)), sem((ITERS + 1, n_c)), sem(()), sem(()),
        ],
        compiler_params=pltpu.CompilerParams(
            collective_id=0, has_side_effects=True, vmem_limit_bytes=48 << 20
        ),
        name="camera_steps",
    )(order, cam_step, wide, cj, pj, res, diag_inverse, coupling)
    return camera, out[:, :, :64].transpose(1, 0, 2)


def solution(mesh):
    in_specs = (
        P(("chain", "pts"), None, None),
        P(("chain", "pts"), None, None),
        P(("chain", "pts"), None, None),
        P(("chain", "pts"), None),
        P(),
        P("chain", None),
        P("chain", None, None),
        P("chain", None, None),
    )
    out_specs = (P("chain", None), P(("chain", "pts"), None, None))
    inner = functools.partial(shards, mesh.shape["chain"], mesh.shape["pts"])
    return jax.shard_map(inner, mesh=mesh, in_specs=in_specs, out_specs=out_specs, check_vma=False)
```
